32 devices in a mesh: replica: 8 (over y, x, core), shard: 4 (over z).
Axes of the slice: x: 2, y: 2, z: 4, core: 2. Of those that a mesh axis runs over, the one named last changes fastest.
Arguments:
- deltas: bfloat16 [8, 131072], P('replica', 'shard'), may hold values from -6 to 6
- counts: int32 [4], replicated, may hold values from 1000 to 8999, as said below
- momentum: float32 [262144], P(('shard', 'replica')), may hold values from -4 to 4
- params: bfloat16 [262144], P(('shard', 'replica')), may hold values from -6 to 6
Outputs:
- new_momentum: float32 [262144], P(('shard', 'replica'))
- new_params: bfloat16 [262144], P('shard')
The draws below stay inside these ranges and needn't reach their ends.
Inputs may be any that keep to these rules, and one draw needn't show every extreme that they name: `counts`: tokens processed by each worker.
All inputs are finite; a program needn't handle non-finite values.
Results may differ from the reference program's by a relative error of at most 0.001.
Values may be sent and summed in bfloat16 or wider, within the bound.
A program may use at most 64 MiB of HBM per device.

```python
import jax
import jax.numpy as jnp
from jax import lax

REPLICAS = 4
TOTAL = 262144
HALF = 131072
N_REPLICA = 8
N_SHARD = 4


def draw_counts(key, part):
    base = jax.random.randint(jax.random.fold_in(key, 11), (REPLICAS,), 1000, 3000)
    steps = jnp.arange(REPLICAS, dtype=jnp.int32)
    rising = (base * (REPLICAS - 1 + 2 * steps) // (REPLICAS - 1)).astype(jnp.int32)
    rising = jnp.where(steps == 0, 1000, rising)
    rising = jnp.where(steps == REPLICAS - 1, 8999, rising)
    return rising.astype(jnp.int32)


def spiked(values, stream_key, source, target, shards_of, factor):
    def block_of(axis_at):
        return (jnp.arange(values.shape[axis_at]) // (values.shape[axis_at] // shards_of)).reshape((-1,) + (1,) * (values.ndim - 1 - axis_at))

    near = jax.random.permutation(stream_key, shards_of)[block_of(target)]
    far = (block_of(target) + shards_of // 2) % shards_of
    return jnp.where((block_of(source) == near) | (block_of(source) == far), factor * values, values)


def level_of(rng, extent, split, smallest, high):
    def one(axis_at, blocks):
        draws = jax.random.uniform(jax.random.fold_in(jax.random.fold_in(rng, 6), axis_at), (blocks,), jnp.float32, smallest / len(split), high / len(split))
        return jnp.repeat(jnp.exp(draws), extent[axis_at] // blocks).reshape((-1,) + (1,) * (len(extent) - axis_at - 1))

    gain = one(*split[0])
    for cut in split[1:]:
        gain = gain * one(*cut)
    return gain


def gaussian(key, shape, deviation, reach, shards=(), held_as=jnp.bfloat16):
    result = jax.random.normal(key, shape, jnp.float32) * deviation
    if len(shards) > 0:
        result = level_of(key, shape, shards, -0.22, 0.18) * result
    return jnp.clip(result, min=-reach, max=reach).astype(held_as)


def gaussian_with(rng, shape, width, reach, cuts, heavy, kind=jnp.bfloat16):
    drawn = width * jax.random.normal(rng, shape, jnp.float32)
    if cuts:
        drawn = drawn * level_of(rng, shape, cuts, -0.22, 0.18)
    return jnp.clip(spiked(drawn, jax.random.fold_in(rng, 3), *heavy), -reach, reach).astype(kind)


def setup_inputs(seed: int = 0) -> dict:
    arg_keys = jax.random.split(jax.random.key(seed), 5)
    return {
        "deltas": gaussian_with(arg_keys[0], (N_REPLICA, HALF), 1.0, 6.0, ((0, 8), (1, 4)), (0, 1, 8, 2.0)),
        "counts": draw_counts(jax.random.fold_in(arg_keys[4], 71), 0),
        "momentum": gaussian(arg_keys[2], (TOTAL,), 0.3, 4.0, ((0, 32),), jnp.float32),
        "params": gaussian(arg_keys[3], (TOTAL,), 1.0, 6.0, ((0, 32),)),
    }


momentum_rate = 0.9
outer_rate = 0.7


def reference(deltas, counts, momentum, params):
    workers = deltas.shape[0] // 2
    stacked = deltas.reshape(workers, 2, N_SHARD, deltas.shape[1] // N_SHARD)
    worker_delta = jnp.transpose(stacked, (0, 2, 1, 3)).reshape(workers, momentum.shape[0])
    shares = counts.astype(jnp.float32)
    shares = shares / jnp.sum(shares)

    def accumulate(total, item):
        row, share = item
        return total + share * row.astype(jnp.float32), None

    outer_grad, _ = lax.scan(accumulate, jnp.zeros((momentum.shape[0],), jnp.float32), (worker_delta, shares))
    new_momentum = momentum_rate * momentum + outer_grad
    new_params = (params.astype(jnp.float32) - outer_rate * (outer_grad + momentum_rate * new_momentum)).astype(jnp.bfloat16)
    return new_momentum, new_params
```

```python
import functools

import jax
import jax.numpy as jnp
from jax import lax
from jax.experimental import pallas as pl
from jax.experimental.pallas import tpu as pltpu
from jax.sharding import PartitionSpec as P

momentum_rate = 0.9
outer_rate = 0.7
LANES = 128


def kernel(
    n, rows, deltas_ref, counts_ref, momentum_ref, params_ref, new_momentum_ref, new_params_ref,
    raw, packed, arrived, mom, par, updated,
    in_sems, own_sem, send_sems, recv_sems, out_send_sems, out_recv_sems,
):
    workers = n // 2
    me = lax.axis_index("replica")
    worker = me // 2
    half = me % 2
    my_half = me // workers

    load_deltas = pltpu.make_async_copy(deltas_ref, raw, in_sems.at[0])
    load_momentum = pltpu.make_async_copy(momentum_ref, mom, in_sems.at[1])
    load_params = pltpu.make_async_copy(params_ref, par, in_sems.at[2])
    load_deltas.start()
    load_momentum.start()
    load_params.start()

    barrier = pltpu.get_barrier_semaphore()
    for step in range(1, n):
        pl.semaphore_signal(
            barrier, inc=1, device_id={"replica": lax.rem(me + step, n)},
            device_id_type=pl.DeviceIdType.MESH,
        )

    load_deltas.wait()
    wide = raw[...].astype(jnp.float32)
    packed[...] = wide.reshape(workers * rows, LANES).astype(jnp.bfloat16)
    pl.semaphore_wait(barrier, n - 1)

    def piece(q):
        return packed.at[pl.ds(pl.multiple_of(q * rows, rows), rows)]

    def slot(r):
        return arrived.at[pl.ds(pl.multiple_of(r * rows, rows), rows)]

    def send(step):
        q = lax.rem(worker + step, workers)
        return half * workers + q, pltpu.make_async_remote_copy(
            src_ref=piece(q), dst_ref=slot(worker), send_sem=send_sems.at[step],
            recv_sem=recv_sems.at[worker], device_id={"replica": half * workers + q},
            device_id_type=pl.DeviceIdType.MESH,
        )

    own = half == my_half
    own_piece = lax.rem(me, workers)
    own_copy = pltpu.make_async_copy(piece(own_piece), slot(worker), own_sem)
    for step in range(workers):
        target, copy = send(step)

        @pl.when(target != me)
        def _():
            copy.start()

    @pl.when(own)
    def _():
        own_copy.start()

    total = counts_ref[0].astype(jnp.float32)
    for r in range(1, workers):
        total = total + counts_ref[r].astype(jnp.float32)
    load_momentum.wait()
    load_params.wait()
    for r in range(workers):
        source = 2 * r + my_half
        recv = pltpu.make_async_remote_copy(
            src_ref=piece(0), dst_ref=slot(r), send_sem=send_sems.at[0],
            recv_sem=recv_sems.at[r], device_id={"replica": source},
            device_id_type=pl.DeviceIdType.MESH,
        )

        @pl.when(source != me)
        def _():
            recv.wait_recv()

        @pl.when(source == me)
        def _():
            own_copy.wait()

    grad = jnp.zeros((rows, LANES), jnp.float32)
    for r in range(workers):
        share = counts_ref[r].astype(jnp.float32) / total
        grad = grad + share * arrived[pl.ds(r * rows, rows)].astype(jnp.float32)
    new_momentum = momentum_rate * mom[...] + grad
    value = (
        par[...].astype(jnp.float32) - outer_rate * (grad + momentum_rate * new_momentum)
    ).astype(jnp.bfloat16)
    updated[...] = value
    new_momentum_ref[...] = new_momentum
    place = pl.ds(pl.multiple_of(me * rows, rows), rows)

    def gather(step):
        return pltpu.make_async_remote_copy(
            src_ref=updated, dst_ref=new_params_ref.at[place], send_sem=out_send_sems.at[step],
            recv_sem=out_recv_sems.at[me], device_id={"replica": lax.rem(me + step, n)},
            device_id_type=pl.DeviceIdType.MESH,
        )

    for step in range(1, n):
        gather(step).start()
    new_params_ref[place] = value

    for step in range(workers):
        target, copy = send(step)

        @pl.when(target != me)
        def _():
            copy.wait_send()

    for step in range(1, n):
        gather(step).wait_send()
    for step in range(1, n):
        source = lax.rem(me + step, n)
        pltpu.make_async_remote_copy(
            src_ref=updated,
            dst_ref=new_params_ref.at[pl.ds(pl.multiple_of(source * rows, rows), rows)],
            send_sem=out_send_sems.at[step], recv_sem=out_recv_sems.at[source],
            device_id={"replica": source}, device_id_type=pl.DeviceIdType.MESH,
        ).wait_recv()


def local(deltas, counts, momentum, params):
    n = lax.axis_size("replica")
    workers = n // 2
    piece_len = momentum.shape[0]
    rows = piece_len // LANES
    new_momentum, new_params = pl.pallas_call(
        functools.partial(kernel, n, rows),
        out_shape=(
            jax.ShapeDtypeStruct((rows, LANES), jnp.float32),
            jax.ShapeDtypeStruct((n * rows, LANES), jnp.bfloat16),
        ),
        in_specs=[
            pl.BlockSpec(memory_space=pl.ANY),
            pl.BlockSpec(memory_space=pltpu.SMEM),
            pl.BlockSpec(memory_space=pl.ANY),
            pl.BlockSpec(memory_space=pl.ANY),
        ],
        out_specs=(
            pl.BlockSpec(memory_space=pltpu.VMEM),
            pl.BlockSpec(memory_space=pltpu.VMEM),
        ),
        scratch_shapes=[
            pltpu.VMEM((1, workers * piece_len), jnp.bfloat16),
            pltpu.VMEM((workers * rows, LANES), jnp.bfloat16),
            pltpu.VMEM((workers * rows, LANES), jnp.bfloat16),
            pltpu.VMEM((rows, LANES), jnp.float32),
            pltpu.VMEM((rows, LANES), jnp.bfloat16),
            pltpu.VMEM((rows, LANES), jnp.bfloat16),
            pltpu.SemaphoreType.DMA((3,)),
            pltpu.SemaphoreType.DMA,
            pltpu.SemaphoreType.DMA((workers,)),
            pltpu.SemaphoreType.DMA((workers,)),
            pltpu.SemaphoreType.DMA((n,)),
            pltpu.SemaphoreType.DMA((n,)),
        ],
        compiler_params=pltpu.CompilerParams(collective_id=0, has_side_effects=True),
    )(deltas, counts, momentum.reshape(rows, LANES), params.reshape(rows, LANES))
    return new_momentum.reshape(piece_len), new_params.reshape(n * piece_len)


def solution(mesh):
    placed = (P("replica", "shard"), P(), P(("shard", "replica")), P(("shard", "replica")))
    return jax.shard_map(
        local,
        mesh=mesh,
        in_specs=placed,
        out_specs=(P(("shard", "replica")), P("shard")),
        check_vma=False,
    )
```

```python
import functools

import jax
import jax.numpy as jnp
from jax import lax
from jax.experimental import pallas as pl
from jax.experimental.pallas import tpu as pltpu
from jax.sharding import PartitionSpec as P

momentum_rate = 0.9
outer_rate = 0.7
LANES = 128


def kernel(
    n, rows, deltas_ref, counts_ref, momentum_ref, params_ref, new_momentum_ref, new_params_ref,
    raw, packed, arrived, mom, par, updated,
    in_sems, own_sem, send_sems, recv_sems, out_send_sems, out_recv_sems,
):
    workers = n // 2
    me = lax.axis_index("replica")
    worker = me // 2
    half = me % 2
    my_half = me // workers

    load_deltas = pltpu.make_async_copy(deltas_ref, raw, in_sems.at[0])
    load_momentum = pltpu.make_async_copy(momentum_ref, mom, in_sems.at[1])
    load_params = pltpu.make_async_copy(params_ref, par, in_sems.at[2])
    load_deltas.start()
    load_momentum.start()
    load_params.start()

    barrier = pltpu.get_barrier_semaphore()
    for step in range(1, n):
        pl.semaphore_signal(
            barrier, inc=1, device_id={"replica": lax.rem(me + step, n)},
            device_id_type=pl.DeviceIdType.MESH,
        )

    load_deltas.wait()
    wide = raw[...].astype(jnp.float32)
    packed[...] = wide.reshape(workers * rows, LANES).astype(jnp.bfloat16)
    pl.semaphore_wait(barrier, n - 1)

    def piece(q):
        return packed.at[pl.ds(pl.multiple_of(q * rows, rows), rows)]

    def slot(r):
        return arrived.at[pl.ds(pl.multiple_of(r * rows, rows), rows)]

    def send(step):
        q = lax.rem(worker + step, workers)
        return half * workers + q, pltpu.make_async_remote_copy(
            src_ref=piece(q), dst_ref=slot(worker), send_sem=send_sems.at[step],
            recv_sem=recv_sems.at[worker], device_id={"replica": half * workers + q},
            device_id_type=pl.DeviceIdType.MESH,
        )

    own = half == my_half
    own_piece = lax.rem(me, workers)
    own_copy = pltpu.make_async_copy(piece(own_piece), slot(worker), own_sem)
    for step in range(workers):
        target, copy = send(step)

        @pl.when(target != me)
        def _():
            copy.start()

    @pl.when(own)
    def _():
        own_copy.start()

    total = counts_ref[0].astype(jnp.float32)
    for r in range(1, workers):
        total = total + counts_ref[r].astype(jnp.float32)
    load_momentum.wait()
    load_params.wait()
    for r in range(workers):
        source = 2 * r + my_half
        recv = pltpu.make_async_remote_copy(
            src_ref=piece(0), dst_ref=slot(r), send_sem=send_sems.at[0],
            recv_sem=recv_sems.at[r], device_id={"replica": source},
            device_id_type=pl.DeviceIdType.MESH,
        )

        @pl.when(source != me)
        def _():
            recv.wait_recv()

        @pl.when(source == me)
        def _():
            own_copy.wait()

    grad = jnp.zeros((rows, LANES), jnp.float32)
    for r in range(workers):
        share = counts_ref[r].astype(jnp.float32) / total
        grad = grad + share * arrived[pl.ds(r * rows, rows)].astype(jnp.float32)
    new_momentum = momentum_rate * mom[...] + grad
    value = (
        par[...].astype(jnp.float32) - outer_rate * (grad + momentum_rate * new_momentum)
    ).astype(jnp.bfloat16)
    updated[...] = value
    new_momentum_ref[...] = new_momentum
    place = pl.ds(pl.multiple_of(me * rows, rows), rows)

    def gather(step):
        return pltpu.make_async_remote_copy(
            src_ref=updated, dst_ref=new_params_ref.at[place], send_sem=out_send_sems.at[step],
            recv_sem=out_recv_sems.at[me], device_id={"replica": lax.rem(me + step, n)},
            device_id_type=pl.DeviceIdType.MESH,
        )

    for step in range(1, n):
        gather(step).start()
    new_params_ref[place] = value

    for step in range(workers):
        target, copy = send(step)

        @pl.when(target != me)
        def _():
            copy.wait_send()

    for step in range(1, n):
        gather(step).wait_send()
    for step in range(1, n):
        source = lax.rem(me + step, n)
        pltpu.make_async_remote_copy(
            src_ref=updated,
            dst_ref=new_params_ref.at[pl.ds(pl.multiple_of(source * rows, rows), rows)],
            send_sem=out_send_sems.at[step], recv_sem=out_recv_sems.at[source],
            device_id={"replica": source}, device_id_type=pl.DeviceIdType.MESH,
        ).wait_recv()


def write_out(momentum_ref, params_ref, new_momentum_ref, new_params_ref, sems):
    first = pltpu.make_async_copy(params_ref, new_params_ref, sems.at[0])
    second = pltpu.make_async_copy(momentum_ref, new_momentum_ref, sems.at[1])
    first.start()
    second.start()
    second.wait()
    first.wait()


def local(deltas, counts, momentum, params):
    n = lax.axis_size("replica")
    workers = n // 2
    piece_len = momentum.shape[0]
    rows = piece_len // LANES
    new_momentum, new_params = pl.pallas_call(
        functools.partial(kernel, n, rows),
        out_shape=(
            pltpu.VMEM((rows, LANES), jnp.float32),
            pltpu.VMEM((n * rows, LANES), jnp.bfloat16),
        ),
        in_specs=[
            pl.BlockSpec(memory_space=pl.ANY),
            pl.BlockSpec(memory_space=pltpu.SMEM),
            pl.BlockSpec(memory_space=pl.ANY),
            pl.BlockSpec(memory_space=pl.ANY),
        ],
        out_specs=(
            pl.BlockSpec(memory_space=pltpu.VMEM),
            pl.BlockSpec(memory_space=pltpu.VMEM),
        ),
        scratch_shapes=[
            pltpu.VMEM((1, workers * piece_len), jnp.bfloat16),
            pltpu.VMEM((workers * rows, LANES), jnp.bfloat16),
            pltpu.VMEM((workers * rows, LANES), jnp.bfloat16),
            pltpu.VMEM((rows, LANES), jnp.float32),
            pltpu.VMEM((rows, LANES), jnp.bfloat16),
            pltpu.VMEM((rows, LANES), jnp.bfloat16),
            pltpu.SemaphoreType.DMA((3,)),
            pltpu.SemaphoreType.DMA,
            pltpu.SemaphoreType.DMA((workers,)),
            pltpu.SemaphoreType.DMA((workers,)),
            pltpu.SemaphoreType.DMA((n,)),
            pltpu.SemaphoreType.DMA((n,)),
        ],
        compiler_params=pltpu.CompilerParams(collective_id=0, has_side_effects=True),
    )(deltas, counts, momentum.reshape(rows, LANES), params.reshape(rows, LANES))
    new_momentum, new_params = pl.pallas_call(
        write_out,
        out_shape=(
            jax.ShapeDtypeStruct((rows, LANES), jnp.float32),
            jax.ShapeDtypeStruct((n * rows, LANES), jnp.bfloat16),
        ),
        in_specs=[pl.BlockSpec(memory_space=pltpu.VMEM)] * 2,
        out_specs=(pl.BlockSpec(memory_space=pl.ANY),) * 2,
        scratch_shapes=[pltpu.SemaphoreType.DMA((2,))],
    )(
        pltpu.with_memory_space_constraint(new_momentum, pltpu.VMEM),
        pltpu.with_memory_space_constraint(new_params, pltpu.VMEM),
    )
    return new_momentum.reshape(piece_len), new_params.reshape(n * piece_len)


def solution(mesh):
    placed = (P("replica", "shard"), P(), P(("shard", "replica")), P(("shard", "replica")))
    return jax.shard_map(
        local,
        mesh=mesh,
        in_specs=placed,
        out_specs=(P(("shard", "replica")), P("shard")),
        check_vma=False,
    )
```

```python
import functools

import jax
import jax.numpy as jnp
from jax import lax
from jax.experimental import pallas as pl
from jax.experimental.pallas import tpu as pltpu
from jax.sharding import PartitionSpec as P

momentum_rate = 0.9
outer_rate = 0.7
LANES = 128
CHUNKS = 1


def flipped(index, mask):
    bit = 1
    while bit <= mask:
        if mask & bit:
            index = index + bit * (1 - 2 * (index // bit % 2))
        bit *= 2
    return index


def far_first(count):
    return sorted(range(count), key=lambda mask: -bin(mask >> 1).count("1"))


def kernel(
    n, rows, deltas_ref, counts_ref, momentum_ref, params_ref, new_momentum_ref, new_params_ref,
    counts, raw, packed, arrived, mom, par,
    in_sems, send_sems, recv_sems, out_send_sems, out_recv_sems,
):
    workers = n // 2
    part = rows // CHUNKS
    me = lax.axis_index("replica")
    worker = me // 2
    half = me % 2
    my_half = me // workers
    my_piece = me % workers

    load_deltas = pltpu.make_async_copy(deltas_ref, raw, in_sems.at[0])
    load_momentum = pltpu.make_async_copy(momentum_ref, mom, in_sems.at[1])
    load_params = pltpu.make_async_copy(params_ref, par, in_sems.at[2])
    load_counts = pltpu.make_async_copy(counts_ref, counts, in_sems.at[3])
    barrier = pltpu.get_barrier_semaphore()
    for mask in far_first(n):
        if mask:
            pl.semaphore_signal(
                barrier, inc=1, device_id={"replica": flipped(me, mask)},
                device_id_type=pl.DeviceIdType.MESH,
            )
    load_deltas.start()
    load_counts.start()
    load_momentum.start()
    load_params.start()

    load_deltas.wait()
    wide = raw[...].astype(jnp.float32)
    packed[...] = wide.reshape(workers * rows, LANES).astype(jnp.bfloat16)

    def span(block, chunk):
        return pl.ds(pl.multiple_of(block * rows + chunk * part, part), part)

    @pl.when(half == my_half)
    def _():
        for chunk in range(CHUNKS):
            arrived[span(worker, chunk)] = packed[span(my_piece, chunk)]

    load_counts.wait()
    total = counts[0].astype(jnp.float32)
    for r in range(1, workers):
        total = total + counts[r].astype(jnp.float32)
    shares = [
        jnp.full((1, LANES), counts[r].astype(jnp.float32)) / jnp.full((1, LANES), total)
        for r in range(workers)
    ]
    load_momentum.wait()
    load_params.wait()
    pl.semaphore_wait(barrier, n - 1)

    def send(mask, chunk):
        q = flipped(my_piece, mask)
        target = half * workers + q
        return target, pltpu.make_async_remote_copy(
            src_ref=packed.at[span(q, chunk)], dst_ref=arrived.at[span(worker, chunk)],
            send_sem=send_sems.at[chunk, mask], recv_sem=recv_sems.at[chunk, worker],
            device_id={"replica": target}, device_id_type=pl.DeviceIdType.MESH,
        )

    def gather(mask, chunk):
        target = flipped(me, mask)
        return pltpu.make_async_remote_copy(
            src_ref=new_params_ref.at[span(me, chunk)], dst_ref=new_params_ref.at[span(me, chunk)],
            send_sem=out_send_sems.at[chunk, mask], recv_sem=out_recv_sems.at[chunk, mask],
            device_id={"replica": target}, device_id_type=pl.DeviceIdType.MESH,
        )

    def landing(mask, chunk):
        source = flipped(me, mask)
        return pltpu.make_async_remote_copy(
            src_ref=new_params_ref.at[span(source, chunk)],
            dst_ref=new_params_ref.at[span(source, chunk)],
            send_sem=out_send_sems.at[chunk, mask], recv_sem=out_recv_sems.at[chunk, mask],
            device_id={"replica": source}, device_id_type=pl.DeviceIdType.MESH,
        )

    for chunk in range(CHUNKS):
        for mask in far_first(workers):
            target, copy = send(mask, chunk)
            if mask:
                copy.start()
            else:

                @pl.when(target != me)
                def _():
                    copy.start()

    for chunk in range(CHUNKS):
        for r in range(workers):
            source = 2 * r + my_half

            @pl.when(source != me)
            def _():
                pltpu.make_async_remote_copy(
                    src_ref=packed.at[span(0, chunk)], dst_ref=arrived.at[span(r, chunk)],
                    send_sem=send_sems.at[chunk, 0], recv_sem=recv_sems.at[chunk, r],
                    device_id={"replica": source}, device_id_type=pl.DeviceIdType.MESH,
                ).wait_recv()

        grad = jnp.zeros((part, LANES), jnp.float32)
        for r in range(workers):
            grad = grad + shares[r] * arrived[span(r, chunk)].astype(jnp.float32)
        own = pl.ds(chunk * part, part)
        new_momentum = momentum_rate * mom[own] + grad
        new_params_ref[span(me, chunk)] = (
            par[own].astype(jnp.float32) - outer_rate * (grad + momentum_rate * new_momentum)
        ).astype(jnp.bfloat16)
        new_momentum_ref[own] = new_momentum
        for mask in far_first(n):
            if mask:
                gather(mask, chunk).start()

    for chunk in range(CHUNKS):
        for mask in far_first(workers):
            target, copy = send(mask, chunk)

            @pl.when(target != me)
            def _():
                copy.wait_send()

    for chunk in range(CHUNKS):
        for mask in range(1, n):
            gather(mask, chunk).wait_send()
    for chunk in range(CHUNKS):
        for mask in range(1, n):
            landing(mask, chunk).wait_recv()


def write_out(momentum_ref, params_ref, new_momentum_ref, new_params_ref, sems):
    first = pltpu.make_async_copy(params_ref, new_params_ref, sems.at[0])
    second = pltpu.make_async_copy(momentum_ref, new_momentum_ref, sems.at[1])
    first.start()
    second.start()
    second.wait()
    first.wait()


def local(deltas, counts, momentum, params):
    n = lax.axis_size("replica")
    workers = n // 2
    piece_len = momentum.shape[0]
    rows = piece_len // LANES
    new_momentum, new_params = pl.pallas_call(
        functools.partial(kernel, n, rows),
        out_shape=(
            pltpu.VMEM((rows, LANES), jnp.float32),
            pltpu.VMEM((n * rows, LANES), jnp.bfloat16),
        ),
        in_specs=[
            pl.BlockSpec(memory_space=pl.ANY),
            pl.BlockSpec(memory_space=pl.ANY),
            pl.BlockSpec(memory_space=pl.ANY),
            pl.BlockSpec(memory_space=pl.ANY),
        ],
        out_specs=(
            pl.BlockSpec(memory_space=pltpu.VMEM),
            pl.BlockSpec(memory_space=pltpu.VMEM),
        ),
        scratch_shapes=[
            pltpu.SMEM((workers,), jnp.int32),
            pltpu.VMEM((1, workers * piece_len), jnp.bfloat16),
            pltpu.VMEM((workers * rows, LANES), jnp.bfloat16),
            pltpu.VMEM((workers * rows, LANES), jnp.bfloat16),
            pltpu.VMEM((rows, LANES), jnp.float32),
            pltpu.VMEM((rows, LANES), jnp.bfloat16),
            pltpu.SemaphoreType.DMA((4,)),
            pltpu.SemaphoreType.DMA((CHUNKS, workers)),
            pltpu.SemaphoreType.DMA((CHUNKS, workers)),
            pltpu.SemaphoreType.DMA((CHUNKS, n)),
            pltpu.SemaphoreType.DMA((CHUNKS, n)),
        ],
        compiler_params=pltpu.CompilerParams(collective_id=0, has_side_effects=True),
    )(deltas, counts, momentum.reshape(rows, LANES), params.reshape(rows, LANES))
    new_momentum, new_params = pl.pallas_call(
        write_out,
        out_shape=(
            jax.ShapeDtypeStruct((rows, LANES), jnp.float32),
            jax.ShapeDtypeStruct((n * rows, LANES), jnp.bfloat16),
        ),
        in_specs=[pl.BlockSpec(memory_space=pltpu.VMEM)] * 2,
        out_specs=(pl.BlockSpec(memory_space=pl.ANY),) * 2,
        scratch_shapes=[pltpu.SemaphoreType.DMA((2,))],
    )(
        pltpu.with_memory_space_constraint(new_momentum, pltpu.VMEM),
        pltpu.with_memory_space_constraint(new_params, pltpu.VMEM),
    )
    return new_momentum.reshape(piece_len), new_params.reshape(n * piece_len)


def solution(mesh):
    placed = (P("replica", "shard"), P(), P(("shard", "replica")), P(("shard", "replica")))
    return jax.shard_map(
        local,
        mesh=mesh,
        in_specs=placed,
        out_specs=(P(("shard", "replica")), P("shard")),
        check_vma=False,
    )
```

```python
import functools

import jax
import jax.numpy as jnp
from jax import lax
from jax.experimental import pallas as pl
from jax.experimental.pallas import tpu as pltpu
from jax.sharding import PartitionSpec as P

momentum_rate = 0.9
outer_rate = 0.7
LANES = 128
CHUNKS = 1


def flipped(index, mask):
    bit = 1
    while bit <= mask:
        if mask & bit:
            index = index + bit * (1 - 2 * (index // bit % 2))
        bit *= 2
    return index


def far_first(count):
    return sorted(range(count), key=lambda mask: -bin(mask >> 1).count("1"))


def kernel(
    n, rows, deltas_ref, counts_ref, momentum_ref, params_ref, new_momentum_ref, new_params_ref,
    counts, raw, packed, arrived, mom, par,
    in_sems, send_sems, recv_sems, out_send_sems, out_recv_sems,
):
    workers = n // 2
    part = rows // CHUNKS
    me = lax.axis_index("replica")
    worker = me // 2
    half = me % 2
    my_half = me // workers
    my_piece = me % workers

    load_deltas = pltpu.make_async_copy(deltas_ref, raw, in_sems.at[0])
    load_momentum = pltpu.make_async_copy(momentum_ref, mom, in_sems.at[1])
    load_params = pltpu.make_async_copy(params_ref, par, in_sems.at[2])
    load_counts = pltpu.make_async_copy(counts_ref, counts, in_sems.at[3])
    barrier = pltpu.get_barrier_semaphore()
    for mask in far_first(n):
        if mask:
            pl.semaphore_signal(
                barrier, inc=1, device_id={"replica": flipped(me, mask)},
                device_id_type=pl.DeviceIdType.MESH,
            )
    load_deltas.start()
    load_counts.start()
    load_momentum.start()
    load_params.start()

    load_deltas.wait()
    wide = raw[...].astype(jnp.float32)
    packed[...] = wide.reshape(workers * rows, LANES).astype(jnp.bfloat16)

    def span(block, chunk):
        return pl.ds(pl.multiple_of(block * rows + chunk * part, part), part)

    @pl.when(half == my_half)
    def _():
        for chunk in range(CHUNKS):
            arrived[span(worker, chunk)] = packed[span(my_piece, chunk)]

    load_counts.wait()
    total = counts[0].astype(jnp.float32)
    for r in range(1, workers):
        total = total + counts[r].astype(jnp.float32)
    shares = [
        jnp.full((1, LANES), counts[flipped(worker, mask)].astype(jnp.float32))
        / jnp.full((1, LANES), total)
        for mask in range(workers)
    ]
    load_momentum.wait()
    load_params.wait()
    pl.semaphore_wait(barrier, n - 1)

    def send(mask, chunk):
        q = flipped(my_piece, mask)
        target = half * workers + q
        return target, pltpu.make_async_remote_copy(
            src_ref=packed.at[span(q, chunk)], dst_ref=arrived.at[span(worker, chunk)],
            send_sem=send_sems.at[chunk, mask], recv_sem=recv_sems.at[chunk, worker],
            device_id={"replica": target}, device_id_type=pl.DeviceIdType.MESH,
        )

    def gather(mask, chunk):
        target = flipped(me, mask)
        return pltpu.make_async_remote_copy(
            src_ref=new_params_ref.at[span(me, chunk)], dst_ref=new_params_ref.at[span(me, chunk)],
            send_sem=out_send_sems.at[chunk, mask], recv_sem=out_recv_sems.at[chunk, mask],
            device_id={"replica": target}, device_id_type=pl.DeviceIdType.MESH,
        )

    def landing(mask, chunk):
        source = flipped(me, mask)
        return pltpu.make_async_remote_copy(
            src_ref=new_params_ref.at[span(source, chunk)],
            dst_ref=new_params_ref.at[span(source, chunk)],
            send_sem=out_send_sems.at[chunk, mask], recv_sem=out_recv_sems.at[chunk, mask],
            device_id={"replica": source}, device_id_type=pl.DeviceIdType.MESH,
        )

    for chunk in range(CHUNKS):
        for mask in far_first(workers):
            target, copy = send(mask, chunk)
            if mask:
                copy.start()
            else:

                @pl.when(target != me)
                def _():
                    copy.start()

    def arrival(mask, chunk):
        r = flipped(worker, mask)
        return pltpu.make_async_remote_copy(
            src_ref=packed.at[span(0, chunk)], dst_ref=arrived.at[span(r, chunk)],
            send_sem=send_sems.at[chunk, 0], recv_sem=recv_sems.at[chunk, r],
            device_id={"replica": 2 * r + my_half}, device_id_type=pl.DeviceIdType.MESH,
        )

    for chunk in range(CHUNKS):
        grad = jnp.zeros((part, LANES), jnp.float32)
        for mask in sorted(range(workers), key=lambda mask: bin(mask).count("1")):
            if mask:
                arrival(mask, chunk).wait_recv()
            else:

                @pl.when(half != my_half)
                def _():
                    arrival(0, chunk).wait_recv()

            grad = grad + shares[mask] * arrived[
                span(flipped(worker, mask), chunk)
            ].astype(jnp.float32)
        own = pl.ds(chunk * part, part)
        new_momentum = momentum_rate * mom[own] + grad
        new_params_ref[span(me, chunk)] = (
            par[own].astype(jnp.float32) - outer_rate * (grad + momentum_rate * new_momentum)
        ).astype(jnp.bfloat16)
        new_momentum_ref[own] = new_momentum
        for mask in far_first(n):
            if mask:
                gather(mask, chunk).start()

    for chunk in range(CHUNKS):
        for mask in far_first(workers):
            target, copy = send(mask, chunk)

            @pl.when(target != me)
            def _():
                copy.wait_send()

    for chunk in range(CHUNKS):
        for mask in range(1, n):
            gather(mask, chunk).wait_send()
    for chunk in range(CHUNKS):
        for mask in range(1, n):
            landing(mask, chunk).wait_recv()


def write_out(momentum_ref, params_ref, new_momentum_ref, new_params_ref, sems):
    first = pltpu.make_async_copy(params_ref, new_params_ref, sems.at[0])
    second = pltpu.make_async_copy(momentum_ref, new_momentum_ref, sems.at[1])
    first.start()
    second.start()
    second.wait()
    first.wait()


def local(deltas, counts, momentum, params):
    n = lax.axis_size("replica")
    workers = n // 2
    piece_len = momentum.shape[0]
    rows = piece_len // LANES
    new_momentum, new_params = pl.pallas_call(
        functools.partial(kernel, n, rows),
        out_shape=(
            pltpu.VMEM((rows, LANES), jnp.float32),
            pltpu.VMEM((n * rows, LANES), jnp.bfloat16),
        ),
        in_specs=[
            pl.BlockSpec(memory_space=pl.ANY),
            pl.BlockSpec(memory_space=pl.ANY),
            pl.BlockSpec(memory_space=pl.ANY),
            pl.BlockSpec(memory_space=pl.ANY),
        ],
        out_specs=(
            pl.BlockSpec(memory_space=pltpu.VMEM),
            pl.BlockSpec(memory_space=pltpu.VMEM),
        ),
        scratch_shapes=[
            pltpu.SMEM((workers,), jnp.int32),
            pltpu.VMEM((1, workers * piece_len), jnp.bfloat16),
            pltpu.VMEM((workers * rows, LANES), jnp.bfloat16),
            pltpu.VMEM((workers * rows, LANES), jnp.bfloat16),
            pltpu.VMEM((rows, LANES), jnp.float32),
            pltpu.VMEM((rows, LANES), jnp.bfloat16),
            pltpu.SemaphoreType.DMA((4,)),
            pltpu.SemaphoreType.DMA((CHUNKS, workers)),
            pltpu.SemaphoreType.DMA((CHUNKS, workers)),
            pltpu.SemaphoreType.DMA((CHUNKS, n)),
            pltpu.SemaphoreType.DMA((CHUNKS, n)),
        ],
        compiler_params=pltpu.CompilerParams(collective_id=0, has_side_effects=True),
    )(deltas, counts, momentum.reshape(rows, LANES), params.reshape(rows, LANES))
    new_momentum, new_params = pl.pallas_call(
        write_out,
        out_shape=(
            jax.ShapeDtypeStruct((rows, LANES), jnp.float32),
            jax.ShapeDtypeStruct((n * rows, LANES), jnp.bfloat16),
        ),
        in_specs=[pl.BlockSpec(memory_space=pltpu.VMEM)] * 2,
        out_specs=(pl.BlockSpec(memory_space=pl.ANY),) * 2,
        scratch_shapes=[pltpu.SemaphoreType.DMA((2,))],
    )(
        pltpu.with_memory_space_constraint(new_momentum, pltpu.VMEM),
        pltpu.with_memory_space_constraint(new_params, pltpu.VMEM),
    )
    return new_momentum.reshape(piece_len), new_params.reshape(n * piece_len)


def solution(mesh):
    placed = (P("replica", "shard"), P(), P(("shard", "replica")), P(("shard", "replica")))
    return jax.shard_map(
        local,
        mesh=mesh,
        in_specs=placed,
        out_specs=(P(("shard", "replica")), P("shard")),
        check_vma=False,
    )
```
